32 devices in a mesh: freq: 4 (over z), tm: 4 (over x, core), grp: 2 (over y).
Axes of the slice: x: 2, y: 2, z: 4, core: 2. Of those that a mesh axis runs over, the one named last changes fastest.
Arguments:
- voltages: bfloat16 [4, 2, 1024, 4096], P(None, None, ('freq', 'grp'), 'tm'), may hold values from -6 to 6
- prior_gains: float32 [4, 2, 1024], P('freq'), may hold values from -4.2 to 4.2
- station_flags: int32 [512], replicated, may hold values 0 or 1
- ingest_map: int32 [512], replicated, may hold values from 0 to 511, each once
- station_coords: float32 [2, 512], replicated, may hold values from -40 to 40
- pointing: int32 [2, 256], replicated, may hold values from 0 to 63
- corr_channels: int32 [4], replicated, may hold values from 0 to 3, each once
- beam_channels: int32 [4], replicated, may hold values from 0 to 3, each once
Outputs:
- visibilities: float32 [4, 2, 1024, 1024], P('freq', None, 'grp', 'tm')
- solved_gains: float32 [4, 2, 1024], P('freq')
- tied_beams: bfloat16 [4, 2, 2, 256, 4096], P('freq', None, None, 'grp', 'tm')
The draws below stay inside these ranges and needn't reach their ends.
Inputs may be any that keep to these rules, and one draw needn't show every extreme that they name: `ingest_map`: each station appears in exactly one ingest slot. `corr_channels`: each channel is handled by exactly one correlator slot. `beam_channels`: each channel is handled by exactly one beamformer slot.
All inputs are finite; a program needn't handle non-finite values.
Results may differ from the reference program's by a relative error of at most 0.0049.
Values may be sent and summed in bfloat16 or wider, within the bound.
A program may use at most 64 MiB of HBM per device.

```python
import math
import jax
import jax.numpy as jnp
from jax import lax

S = 512
NBEAM = 256
ITERS = 4
NIN = 1024
C = 4
TIME = 4096


def plant(drawn, rng, least, top_value):
    spot = [jax.random.randint(jax.random.fold_in(rng, axis), (), 0, length) for axis, length in enumerate(drawn.shape)]
    longest = drawn.shape.index(max(drawn.shape))
    beside = spot[:longest] + [(spot[longest] + 1) % drawn.shape[longest]] + spot[longest + 1:]
    return drawn.at[tuple(spot)].set(least).at[tuple(beside)].set(top_value)


def block_levels(stream_key, dims, pieces, low, top_value):
    gain, own = 1.0, jax.random.fold_in(stream_key, 6)
    for position, parts in pieces:
        heights = jnp.exp(jax.random.uniform(jax.random.fold_in(own, position), (parts,), jnp.float32, low / len(pieces), top_value / len(pieces)))
        gain = gain * jnp.repeat(heights, dims[position] // parts).reshape([-1 if axis == position else 1 for axis in range(len(dims))])
    return gain


def gaussian(stream_key, dims, spread, most, shards=(), held_as=jnp.bfloat16):
    array = spread * jax.random.normal(stream_key, dims, jnp.float32)
    if shards:
        array = array * block_levels(stream_key, dims, shards, -0.22, 0.18)
    return jnp.clip(array, -most, most).astype(held_as)


def setup_inputs(seed: int = 0) -> dict:
    keys = jax.random.split(jax.random.key(seed), 9)
    return {
        "voltages": gaussian(keys[0], (C, 2, NIN, TIME), 1.0, 6.0, ((2, 8), (3, 4))),
        "prior_gains": gaussian(keys[1], (C, 2, NIN), 0.7, 4.2, ((0, 4),), jnp.float32),
        "station_flags": plant((jax.random.randint(keys[2], (S,), 0, 16) < 1).astype(jnp.int32), jax.random.fold_in(keys[2], 1), 0, 1),
        "ingest_map": jax.random.permutation(keys[3], S).astype(jnp.int32),
        "station_coords": jnp.clip(jax.random.uniform(keys[4], (2, S), jnp.float32, -40.0, 40.0), -40.0, 40.0),
        "pointing": plant(jax.random.randint(keys[5], (2, NBEAM), 0, 64), jax.random.fold_in(keys[5], 1), 0, 63).astype(jnp.int32),
        "corr_channels": jax.random.permutation(keys[6], C).astype(jnp.int32),
        "beam_channels": jax.random.permutation(keys[7], C).astype(jnp.int32),
    }


grid_cells = 64.0

def keep_inputs(station_flags, ingest_map):
    slot_keep = 1 - jnp.take(station_flags, ingest_map)
    return jnp.concatenate([slot_keep, slot_keep]).astype(jnp.bfloat16)

def correlate(block):
    left_real = jnp.concatenate([block[0], block[1]], axis=1)
    left_imag = jnp.concatenate([block[1], -block[0]], axis=1)
    real_part = jnp.dot(left_real, left_real.T, preferred_element_type=jnp.float32)
    imag_part = jnp.dot(left_imag, left_real.T, preferred_element_type=jnp.float32)
    return jnp.stack([real_part, imag_part]) * (1.0 / TIME)

def solve(visibilities, prior_gains):
    gains = prior_gains
    highest = lax.Precision.HIGHEST
    for iteration in range(ITERS):
        power = lax.optimization_barrier(jnp.sum(gains * gains, axis=(1, 2))) + 1e-06
        real_real = jnp.einsum('cij,cj->ci', visibilities[:, 0], gains[:, 0], precision=highest)
        imag_imag = jnp.einsum('cij,cj->ci', visibilities[:, 1], gains[:, 1], precision=highest)
        real_imag = jnp.einsum('cij,cj->ci', visibilities[:, 0], gains[:, 1], precision=highest)
        imag_real = jnp.einsum('cij,cj->ci', visibilities[:, 1], gains[:, 0], precision=highest)
        update = jnp.stack([real_real - imag_imag, imag_real + real_imag], axis=1)
        gains = 0.5 * (gains + 2 * S * update / power[:, None, None])
    return gains

def weights_for(gains_sel, ratio, pointing_part, slot_coords):
    east_dir = (pointing_part[0].astype(jnp.float32) + 0.5) / grid_cells - 0.5
    north_dir = (pointing_part[1].astype(jnp.float32) + 0.5) / grid_cells - 0.5
    phase = 2.0 * math.pi * ratio * (east_dir[:, None] * slot_coords[0][None, :] + north_dir[:, None] * slot_coords[1][None, :])
    cosine = jnp.cos(phase)
    sine = jnp.sin(phase)
    gain_real = gains_sel[0].reshape(2, S)
    gain_imag = gains_sel[1].reshape(2, S)
    denom = jnp.maximum(gain_real * gain_real + gain_imag * gain_imag, 0.5)
    along_real = gain_real / denom
    along_imag = gain_imag / denom
    factor = 1.0 / math.sqrt(S)
    w_real = (cosine[None] * along_real[:, None, :] - sine[None] * along_imag[:, None, :]) * factor
    w_imag = -(cosine[None] * along_imag[:, None, :] + sine[None] * along_real[:, None, :]) * factor
    upper = jnp.stack([w_real, -w_imag], axis=2)
    lower = jnp.stack([w_imag, w_real], axis=2)
    return jnp.stack([upper, lower], axis=1).astype(jnp.bfloat16)

def reference(voltages, prior_gains, station_flags, ingest_map, station_coords, pointing, corr_channels, beam_channels):
    keep = keep_inputs(station_flags, ingest_map)

    def corr_slot(channel):
        block = voltages[channel] * keep[None, :, None]
        return correlate(block)
    visibilities = lax.map(corr_slot, corr_channels)
    solved = solve(visibilities, prior_gains)
    slot_coords = jnp.take(station_coords, ingest_map, axis=1)

    def beam_slot(channel):
        onehot = (corr_channels == channel).astype(jnp.float32)
        gains_sel = jnp.einsum('k,kri->ri', onehot, solved, precision=lax.Precision.HIGHEST)
        ratio = 0.875 + 0.25 * (channel.astype(jnp.float32) + 0.5) / C
        weights = weights_for(gains_sel, ratio, pointing, slot_coords)
        block = (voltages[channel] * keep[None, :, None]).reshape(2, 2, S, TIME)
        beams = jnp.einsum('pobrq,rpqt->pobt', weights.astype(jnp.float32), block.astype(jnp.float32))
        return beams.astype(jnp.bfloat16)
    tied_beams = lax.map(beam_slot, beam_channels)
    return (visibilities, solved, tied_beams)
```

```python
import functools
import math

import jax
import jax.numpy as jnp
from jax import lax
from jax.experimental import pallas as pl
from jax.experimental.pallas import tpu as pltpu
from jax.sharding import PartitionSpec as P

ITERS = 4
LANES = 128
grid_cells = 64.0
MESH = pl.DeviceIdType.MESH


def partner(index, mask, count):
    result, bit = 0, 1
    while bit < count:
        digit = (index // bit) % 2
        result = result + bit * ((1 - digit) if mask & bit else digit)
        bit *= 2
    return result


def nt_dot(a, b):
    return lax.dot_general(a, b, (((1,), (1,)), ((), ())), preferred_element_type=jnp.float32)


def kernel(
    nf,
    nt,
    ng,
    chunks,
    src_c,
    src_b,
    prior,
    onehot,
    cosine,
    sine,
    vis_out,
    gains_out,
    beams_out,
    corr,
    beam,
    gram,
    stage,
    landed,
    updates,
    z,
    gains,
    zs,
    zr,
    ys,
    yr,
    own_sem,
    vs,
    vr,
    us,
    ur,
    gs,
    gr,
):
    f = lax.axis_index("freq")
    t = lax.axis_index("tm")
    g = lax.axis_index("grp")
    _, _, per_input, samples = src_c.shape
    inputs = nf * ng * per_input
    rows = inputs // ng
    cols = inputs // nt
    half = inputs // 2
    offsets = [(dt, dg) for dg in range(ng) for dt in range(nt) if (dt, dg) != (0, 0)]
    masks = list(range(nf - 1, 0, -1))
    peers = {k: partner(f, k, nf) for k in range(nf)}

    def group(dt, dg):
        return {"freq": f, "tm": (t + dt) % nt, "grp": (g + dg) % ng}

    def along_freq(k):
        return {"freq": peers[k], "tm": t, "grp": g}

    barrier = pltpu.get_barrier_semaphore()
    for k in masks:
        pl.semaphore_signal(barrier, inc=1, device_id=along_freq(k), device_id_type=MESH)
    for dt, dg in offsets:
        pl.semaphore_signal(barrier, inc=1, device_id=group(dt, dg), device_id_type=MESH)
    pl.semaphore_wait(barrier, len(masks) + len(offsets))

    sources = (src_c, src_b)
    wholes = (corr, beam)

    def place(whole, owner, chunk):
        part, first, count = chunk
        start = pl.multiple_of((owner * ng + g) * per_input + first, count)
        return whole.at[part, pl.ds(start, count), :]

    def z_copy(which, k, ci):
        part, first, count = chunks[ci]
        return pltpu.make_async_remote_copy(
            src_ref=sources[which].at[peers[k], part, pl.ds(first, count), :],
            dst_ref=place(wholes[which], f, chunks[ci]),
            send_sem=zs.at[which, k - 1, ci],
            recv_sem=zr.at[which, k - 1, ci],
            device_id=along_freq(k),
            device_id_type=MESH,
        )

    def y_copy(which, k, ci, dg):
        part, first, count = chunks[ci]
        spot = place(wholes[which], peers[k], chunks[ci])
        origin = sources[which].at[f, part, pl.ds(first, count), :] if k == 0 else spot
        return pltpu.make_async_remote_copy(
            src_ref=origin,
            dst_ref=spot,
            send_sem=ys.at[which, dg - 1, k, ci],
            recv_sem=yr.at[which, dg - 1, k, ci],
            device_id=group(0, dg),
            device_id_type=MESH,
        )

    def forward(which, k, ci):
        for dg in range(1, ng):
            y_copy(which, k, ci, dg).start()

    def own_copy(which):
        start = pl.multiple_of((f * ng + g) * per_input, per_input)
        return pltpu.make_async_copy(
            sources[which].at[f], wholes[which].at[:, pl.ds(start, per_input), :], own_sem.at[which]
        )

    all_chunks = range(len(chunks))
    for which in (0, 1):
        for ci in all_chunks:
            for k in masks:
                z_copy(which, k, ci).start()
        if which == 0:
            for ci in all_chunks:
                forward(0, 0, ci)
    own_copy(0).start()
    own_copy(1).start()
    for ci in all_chunks:
        for k in masks:
            z_copy(0, k, ci).wait_recv()
            forward(0, k, ci)
    for ci in all_chunks:
        forward(1, 0, ci)
    own_copy(0).wait()
    for ci in all_chunks:
        for k in range(nf):
            for dg in range(1, ng):
                y_copy(0, k, ci, dg).wait_recv()

    scale = 1.0 / (samples * nt)
    row_start = pl.multiple_of(g * rows, rows)

    def vis_copy(i):
        return pltpu.make_async_remote_copy(
            src_ref=stage.at[i],
            dst_ref=landed.at[i],
            send_sem=vs.at[i],
            recv_sem=vr.at[i],
            device_id=group(i + 1, 0),
            device_id_type=MESH,
        )

    def correlate(i, carry):
        j = (t + 1 + i) % nt
        tile = pl.ds(pl.multiple_of(j * cols, cols), cols)
        mine_r = corr[0, pl.ds(row_start, rows), :]
        mine_i = corr[1, pl.ds(row_start, rows), :]
        other_r = corr[0, tile, :]
        other_i = corr[1, tile, :]
        real = (nt_dot(mine_r, other_r) + nt_dot(mine_i, other_i)) * scale
        imag = (nt_dot(mine_i, other_r) - nt_dot(mine_r, other_i)) * scale
        gram[0, :, tile] = real
        gram[1, :, tile] = imag

        @pl.when(i < nt - 1)
        def _():
            stage[i, 0] = real.astype(jnp.bfloat16)
            stage[i, 1] = imag.astype(jnp.bfloat16)
            vis_copy(i).start()

        return carry

    lax.fori_loop(0, nt, correlate, 0)

    pending = [(k, ci) for ci in all_chunks for k in masks]
    share = -(-len(pending) // (ITERS + 1))

    def relay(step):
        for k, ci in pending[step * share : (step + 1) * share]:
            z_copy(1, k, ci).wait_recv()
            forward(1, k, ci)

    z[...] = prior[0]
    slot = g * nt + t
    strip = LANES

    def update_copy(iteration, o):
        dt, dg = offsets[o]
        return pltpu.make_async_remote_copy(
            src_ref=updates.at[iteration, slot],
            dst_ref=updates.at[iteration, slot],
            send_sem=us.at[iteration, o],
            recv_sem=ur.at[iteration, o],
            device_id=group(dt, dg),
            device_id_type=MESH,
        )

    for iteration in range(ITERS):
        relay(iteration)
        power = jnp.sum(z[...] * z[...]) + 1e-06

        def product(r, carry):
            here = pl.ds(pl.multiple_of(r * strip, strip), strip)
            total_r = jnp.zeros((strip, LANES), jnp.float32)
            total_i = jnp.zeros((strip, LANES), jnp.float32)
            for c in range(inputs // LANES):
                lanes = slice(c * LANES, (c + 1) * LANES)
                part_r = gram[0, here, lanes]
                part_i = gram[1, here, lanes]
                gain_r = z[0:1, lanes]
                gain_i = z[1:2, lanes]
                total_r += part_r * gain_r - part_i * gain_i
                total_i += part_i * gain_r + part_r * gain_i
            updates[iteration, slot, 0:1, here] = jnp.sum(total_r.T, axis=0, keepdims=True)
            updates[iteration, slot, 1:2, here] = jnp.sum(total_i.T, axis=0, keepdims=True)
            return carry

        lax.fori_loop(0, rows // strip, product, 0)
        for o in range(len(offsets)):
            update_copy(iteration, o).start()
        for o in range(len(offsets)):
            update_copy(iteration, o).wait_recv()
        for h in range(ng):
            total = updates[iteration, h * nt]
            for other in range(1, nt):
                total = total + updates[iteration, h * nt + other]
            lanes = slice(h * rows, (h + 1) * rows)
            z[:, lanes] = 0.5 * (z[:, lanes] + inputs * total / power)

    gains[f] = z[...]
    gains_out[0] = z[...]

    def gain_copy(k):
        return pltpu.make_async_remote_copy(
            src_ref=gains.at[f],
            dst_ref=gains.at[f],
            send_sem=gs.at[k - 1],
            recv_sem=gr.at[k - 1],
            device_id=along_freq(k),
            device_id_type=MESH,
        )

    for k in masks:
        gain_copy(k).start()
    relay(ITERS)
    for k in masks:
        gain_copy(k).wait_recv()

    for i in range(nt - 1):
        vis_copy(i).wait_recv()
    own_tile = pl.ds(pl.multiple_of(t * cols, cols), cols)
    for part in (0, 1):
        total = gram[part, :, own_tile]
        for i in range(nt - 1):
            total = total + landed[i, part].astype(jnp.float32)
        vis_out[0, part] = total

    selected = onehot[0] * gains[0]
    for k in range(1, nf):
        selected = selected + onehot[k] * gains[k]

    own_copy(1).wait()
    for ci in all_chunks:
        for k in range(nf):
            for dg in range(1, ng):
                y_copy(1, k, ci, dg).wait_recv()

    beams = cosine.shape[0]
    factor = 1.0 / math.sqrt(half)
    cos = cosine[...]
    sin = sine[...]
    for p in (0, 1):
        gain_r = selected[0:1, p * half : (p + 1) * half]
        gain_i = selected[1:2, p * half : (p + 1) * half]
        denom = jnp.maximum(gain_r * gain_r + gain_i * gain_i, 0.5)
        along_r = gain_r / denom
        along_i = gain_i / denom
        w_r = (cos * along_r - sin * along_i) * factor
        w_i = -(cos * along_i + sin * along_r) * factor
        left = jnp.concatenate([w_r, w_i], axis=0).astype(jnp.bfloat16)
        right = jnp.concatenate([-w_i, w_r], axis=0).astype(jnp.bfloat16)
        result = jnp.dot(left, beam[0, p * half : (p + 1) * half, :], preferred_element_type=jnp.float32)
        result += jnp.dot(right, beam[1, p * half : (p + 1) * half, :], preferred_element_type=jnp.float32)
        result = result.astype(jnp.bfloat16)
        beams_out[0, p, 0] = result[:beams]
        beams_out[0, p, 1] = result[beams:]

    for which in (0, 1):
        for ci in all_chunks:
            for k in masks:
                z_copy(which, k, ci).wait_send()
            for k in range(nf):
                for dg in range(1, ng):
                    y_copy(which, k, ci, dg).wait_send()
    for i in range(nt - 1):
        vis_copy(i).wait_send()
    for iteration in range(ITERS):
        for o in range(len(offsets)):
            update_copy(iteration, o).wait_send()
    for k in masks:
        gain_copy(k).wait_send()


def body(
    voltages,
    prior_gains,
    station_flags,
    ingest_map,
    station_coords,
    pointing,
    corr_channels,
    beam_channels,
):
    nf = lax.axis_size("freq")
    nt = lax.axis_size("tm")
    ng = lax.axis_size("grp")
    f = lax.axis_index("freq")
    g = lax.axis_index("grp")
    channels, _, per_input, samples = voltages.shape
    stations = ingest_map.shape[0]
    inputs = 2 * stations
    rows, cols = inputs // ng, inputs // nt
    slot_keep = 1 - jnp.take(station_flags, ingest_map)
    keep = jnp.concatenate([slot_keep, slot_keep]).astype(jnp.bfloat16)
    mine = lax.dynamic_slice_in_dim(keep, (f * ng + g) * per_input, per_input)
    src_c = jnp.take(voltages, corr_channels, axis=0) * mine[None, None, :, None]
    src_b = jnp.take(voltages, beam_channels, axis=0) * mine[None, None, :, None]
    my_beam = lax.dynamic_slice_in_dim(beam_channels, f, 1, 0)
    onehot = (corr_channels == my_beam).astype(jnp.float32)
    ratio = 0.875 + 0.25 * (my_beam.astype(jnp.float32) + 0.5) / channels
    n_beams = pointing.shape[1] // ng
    pointing_part = lax.dynamic_slice_in_dim(pointing, g * n_beams, n_beams, 1)
    slot_coords = jnp.take(station_coords, ingest_map, axis=1)
    east = (pointing_part[0].astype(jnp.float32) + 0.5) / grid_cells - 0.5
    north = (pointing_part[1].astype(jnp.float32) + 0.5) / grid_cells - 0.5
    phase = 2.0 * math.pi * ratio * (
        east[:, None] * slot_coords[0][None, :] + north[:, None] * slot_coords[1][None, :]
    )
    step = min(per_input, 64)
    chunks = tuple((part, first, step) for first in range(0, per_input, step) for part in (0, 1))
    nc = len(chunks)
    dma = pltpu.SemaphoreType.DMA
    vmem = pl.BlockSpec(memory_space=pltpu.VMEM)
    vis, gains, beams = pl.pallas_call(
        functools.partial(kernel, nf, nt, ng, chunks),
        out_shape=(
            jax.ShapeDtypeStruct((1, 2, rows, cols), jnp.float32),
            jax.ShapeDtypeStruct((1, 2, inputs), jnp.float32),
            jax.ShapeDtypeStruct((1, 2, 2, n_beams, samples), jnp.bfloat16),
        ),
        in_specs=[vmem, vmem, vmem, pl.BlockSpec(memory_space=pltpu.SMEM), vmem, vmem],
        out_specs=(vmem, vmem, vmem),
        scratch_shapes=[
            pltpu.VMEM((2, inputs, samples), jnp.bfloat16),
            pltpu.VMEM((2, inputs, samples), jnp.bfloat16),
            pltpu.VMEM((2, rows, inputs), jnp.float32),
            pltpu.VMEM((nt, 2, rows, cols), jnp.bfloat16),
            pltpu.VMEM((nt - 1, 2, rows, cols), jnp.bfloat16),
            pltpu.VMEM((ITERS, ng * nt, 2, rows), jnp.float32),
            pltpu.VMEM((2, inputs), jnp.float32),
            pltpu.VMEM((nf, 2, inputs), jnp.float32),
            dma((2, nf - 1, nc)),
            dma((2, nf - 1, nc)),
            dma((2, ng - 1, nf, nc)),
            dma((2, ng - 1, nf, nc)),
            dma((2,)),
            dma((nt - 1,)),
            dma((nt - 1,)),
            dma((ITERS, ng * nt - 1)),
            dma((ITERS, ng * nt - 1)),
            dma((nf - 1,)),
            dma((nf - 1,)),
        ],
        compiler_params=pltpu.CompilerParams(
            collective_id=0, has_side_effects=True, vmem_limit_bytes=48 * 1024 * 1024
        ),
    )(src_c, src_b, prior_gains, onehot, jnp.cos(phase), jnp.sin(phase))
    return vis, gains, beams


def solution(mesh):
    return jax.shard_map(
        body,
        mesh=mesh,
        in_specs=(
            P(None, None, ("freq", "grp"), "tm"),
            P("freq", None, None),
            P(),
            P(),
            P(),
            P(),
            P(),
            P(),
        ),
        out_specs=(
            P("freq", None, "grp", "tm"),
            P("freq", None, None),
            P("freq", None, None, "grp", "tm"),
        ),
        check_vma=False,
    )
```

```python
import functools
import math

import jax
import jax.numpy as jnp
from jax import lax
from jax.experimental import pallas as pl
from jax.experimental.pallas import tpu as pltpu
from jax.sharding import PartitionSpec as P

ITERS = 4
LANES = 128
grid_cells = 64.0
MESH = pl.DeviceIdType.MESH


def partner(index, mask, count):
    result, bit = 0, 1
    while bit < count:
        digit = (index // bit) % 2
        result = result + bit * ((1 - digit) if mask & bit else digit)
        bit *= 2
    return result


def nt_dot(a, b):
    return lax.dot_general(a, b, (((1,), (1,)), ((), ())), preferred_element_type=jnp.float32)


def kernel(
    nf,
    nt,
    ng,
    chunks,
    voltages,
    prior,
    flags,
    slots,
    coords,
    pointing,
    corr_channels,
    beam_channels,
    vis_out,
    gains_out,
    beams_out,
    src_c,
    src_b,
    keep,
    cosine,
    sine,
    corr,
    beam,
    gram,
    stage,
    landed,
    updates,
    z,
    gains,
    zs,
    zr,
    ys,
    yr,
    own_sem,
    vs,
    vr,
    us,
    ur,
    gs,
    gr,
):
    f = lax.axis_index("freq")
    t = lax.axis_index("tm")
    g = lax.axis_index("grp")
    _, _, per_input, samples = voltages.shape
    inputs = nf * ng * per_input
    rows = inputs // ng
    cols = inputs // nt
    half = inputs // 2
    offsets = [(dt, dg) for dg in range(ng) for dt in range(nt) if (dt, dg) != (0, 0)]
    masks = list(range(nf - 1, 0, -1))
    peers = {k: partner(f, k, nf) for k in range(nf)}

    def group(dt, dg):
        return {"freq": f, "tm": (t + dt) % nt, "grp": (g + dg) % ng}

    def along_freq(k):
        return {"freq": peers[k], "tm": t, "grp": g}

    stations = half
    slot_rows = jnp.broadcast_to(slots[...].astype(jnp.float32), (LANES, stations)).T
    flagged = jnp.zeros((stations, LANES), jnp.float32)
    for first in range(0, stations, LANES):
        lane = lax.broadcasted_iota(jnp.int32, (stations, LANES), 1) + first
        flag = flags[0:1, first : first + LANES].astype(jnp.float32)
        flagged += jnp.where(slot_rows == lane.astype(jnp.float32), flag, 0.0)
    flagged = jnp.sum(flagged, axis=1, keepdims=True)
    keep[...] = jnp.broadcast_to(1.0 - flagged, (stations, LANES))

    barrier = pltpu.get_barrier_semaphore()
    for k in masks:
        pl.semaphore_signal(barrier, inc=1, device_id=along_freq(k), device_id_type=MESH)
    for dt, dg in offsets:
        pl.semaphore_signal(barrier, inc=1, device_id=group(dt, dg), device_id_type=MESH)
    first_slot = pl.multiple_of(((f * ng + g) * per_input) % stations, per_input)
    kept = keep[pl.ds(first_slot, per_input), 0:1].astype(jnp.bfloat16)

    def pick(source, channels):
        for k in masks + [0]:
            for part in (0, 1):
                source[peers[k], part] = voltages[channels[peers[k]], part] * kept

    pick(src_c, corr_channels)
    pl.semaphore_wait(barrier, len(masks) + len(offsets))

    sources = (src_c, src_b)
    wholes = (corr, beam)

    def place(whole, owner, chunk):
        part, first, count = chunk
        start = pl.multiple_of((owner * ng + g) * per_input + first, count)
        return whole.at[part, pl.ds(start, count), :]

    def z_copy(which, k, ci):
        part, first, count = chunks[ci]
        return pltpu.make_async_remote_copy(
            src_ref=sources[which].at[peers[k], part, pl.ds(first, count), :],
            dst_ref=place(wholes[which], f, chunks[ci]),
            send_sem=zs.at[which, k - 1, ci],
            recv_sem=zr.at[which, k - 1, ci],
            device_id=along_freq(k),
            device_id_type=MESH,
        )

    def y_copy(which, k, ci, dg):
        part, first, count = chunks[ci]
        spot = place(wholes[which], peers[k], chunks[ci])
        origin = sources[which].at[f, part, pl.ds(first, count), :] if k == 0 else spot
        return pltpu.make_async_remote_copy(
            src_ref=origin,
            dst_ref=spot,
            send_sem=ys.at[which, dg - 1, k, ci],
            recv_sem=yr.at[which, dg - 1, k, ci],
            device_id=group(0, dg),
            device_id_type=MESH,
        )

    def forward(which, k, ci):
        for dg in range(1, ng):
            y_copy(which, k, ci, dg).start()

    def own_copy(which):
        start = pl.multiple_of((f * ng + g) * per_input, per_input)
        return pltpu.make_async_copy(
            sources[which].at[f], wholes[which].at[:, pl.ds(start, per_input), :], own_sem.at[which]
        )

    beams = cosine.shape[0]
    my_beam = beam_channels[f]

    def point_phases():
        ratio = 0.875 + 0.25 * (my_beam.astype(jnp.float32) + 0.5) / nf
        here = pl.ds(pl.multiple_of(g * beams, beams), beams)
        east_dir, north_dir = (
            jnp.broadcast_to((pointing[d : d + 1, here].astype(jnp.float32) + 0.5) / grid_cells - 0.5, (LANES, beams)).T
            for d in (0, 1)
        )
        east, north = (jnp.broadcast_to(coords[d : d + 1, :], (LANES, stations)).T for d in (0, 1))
        station = lax.broadcasted_iota(jnp.int32, (stations, LANES), 0)
        for first in range(0, stations, LANES):
            lanes = slice(first, first + LANES)
            match = station == slots[0:1, lanes]
            slot_east = jnp.sum(jnp.where(match, east, 0.0), axis=0, keepdims=True)
            slot_north = jnp.sum(jnp.where(match, north, 0.0), axis=0, keepdims=True)
            phase = 2.0 * math.pi * ratio * (east_dir * slot_east + north_dir * slot_north)
            cosine[:, lanes] = jnp.cos(phase)
            sine[:, lanes] = jnp.sin(phase)

    all_chunks = range(len(chunks))
    for ci in all_chunks:
        for k in masks:
            z_copy(0, k, ci).start()
    for ci in all_chunks:
        forward(0, 0, ci)
    own_copy(0).start()
    pick(src_b, beam_channels)
    point_phases()
    for ci in all_chunks:
        for k in masks:
            z_copy(1, k, ci).start()
    own_copy(1).start()
    for ci in all_chunks:
        for k in masks:
            z_copy(0, k, ci).wait_recv()
            forward(0, k, ci)
    for ci in all_chunks:
        forward(1, 0, ci)
    own_copy(0).wait()
    for ci in all_chunks:
        for k in range(nf):
            for dg in range(1, ng):
                y_copy(0, k, ci, dg).wait_recv()

    scale = 1.0 / (samples * nt)
    row_start = pl.multiple_of(g * rows, rows)

    def vis_copy(i):
        return pltpu.make_async_remote_copy(
            src_ref=stage.at[i],
            dst_ref=landed.at[i],
            send_sem=vs.at[i],
            recv_sem=vr.at[i],
            device_id=group(i + 1, 0),
            device_id_type=MESH,
        )

    def correlate(i, carry):
        j = (t + 1 + i) % nt
        tile = pl.ds(pl.multiple_of(j * cols, cols), cols)
        mine_r = corr[0, pl.ds(row_start, rows), :]
        mine_i = corr[1, pl.ds(row_start, rows), :]
        other_r = corr[0, tile, :]
        other_i = corr[1, tile, :]
        real = (nt_dot(mine_r, other_r) + nt_dot(mine_i, other_i)) * scale
        imag = (nt_dot(mine_i, other_r) - nt_dot(mine_r, other_i)) * scale
        gram[0, :, tile] = real
        gram[1, :, tile] = imag

        @pl.when(i < nt - 1)
        def _():
            stage[i, 0] = real.astype(jnp.bfloat16)
            stage[i, 1] = imag.astype(jnp.bfloat16)
            vis_copy(i).start()

        return carry

    lax.fori_loop(0, nt, correlate, 0)

    pending = [(k, ci) for ci in all_chunks for k in masks]
    share = -(-len(pending) // (ITERS + 1))

    def relay(step):
        for k, ci in pending[step * share : (step + 1) * share]:
            z_copy(1, k, ci).wait_recv()
            forward(1, k, ci)

    z[...] = prior[0]
    slot = g * nt + t
    strip = LANES

    def update_copy(iteration, o):
        dt, dg = offsets[o]
        return pltpu.make_async_remote_copy(
            src_ref=updates.at[iteration, slot],
            dst_ref=updates.at[iteration, slot],
            send_sem=us.at[iteration, o],
            recv_sem=ur.at[iteration, o],
            device_id=group(dt, dg),
            device_id_type=MESH,
        )

    for iteration in range(ITERS):
        relay(iteration)
        power = jnp.sum(z[...] * z[...]) + 1e-06

        def product(r, carry):
            here = pl.ds(pl.multiple_of(r * strip, strip), strip)
            total_r = jnp.zeros((strip, LANES), jnp.float32)
            total_i = jnp.zeros((strip, LANES), jnp.float32)
            for c in range(inputs // LANES):
                lanes = slice(c * LANES, (c + 1) * LANES)
                part_r = gram[0, here, lanes]
                part_i = gram[1, here, lanes]
                gain_r = z[0:1, lanes]
                gain_i = z[1:2, lanes]
                total_r += part_r * gain_r - part_i * gain_i
                total_i += part_i * gain_r + part_r * gain_i
            updates[iteration, slot, 0:1, here] = jnp.sum(total_r.T, axis=0, keepdims=True)
            updates[iteration, slot, 1:2, here] = jnp.sum(total_i.T, axis=0, keepdims=True)
            return carry

        lax.fori_loop(0, rows // strip, product, 0)
        for o in range(len(offsets)):
            update_copy(iteration, o).start()
        for o in range(len(offsets)):
            update_copy(iteration, o).wait_recv()
        for h in range(ng):
            total = updates[iteration, h * nt]
            for other in range(1, nt):
                total = total + updates[iteration, h * nt + other]
            lanes = slice(h * rows, (h + 1) * rows)
            z[:, lanes] = 0.5 * (z[:, lanes] + inputs * total / power)

    gains[f] = z[...]
    gains_out[0] = z[...]

    def gain_copy(k):
        return pltpu.make_async_remote_copy(
            src_ref=gains.at[f],
            dst_ref=gains.at[f],
            send_sem=gs.at[k - 1],
            recv_sem=gr.at[k - 1],
            device_id=along_freq(k),
            device_id_type=MESH,
        )

    for k in masks:
        gain_copy(k).start()
    relay(ITERS)
    for k in masks:
        gain_copy(k).wait_recv()

    for i in range(nt - 1):
        vis_copy(i).wait_recv()
    own_tile = pl.ds(pl.multiple_of(t * cols, cols), cols)
    for part in (0, 1):
        total = gram[part, :, own_tile]
        for i in range(nt - 1):
            total = total + landed[i, part].astype(jnp.float32)
        vis_out[0, part] = total

    selected = jnp.zeros_like(z)
    for k in range(nf):
        selected = selected + jnp.where(corr_channels[k] == my_beam, 1.0, 0.0) * gains[k]

    own_copy(1).wait()
    for ci in all_chunks:
        for k in range(nf):
            for dg in range(1, ng):
                y_copy(1, k, ci, dg).wait_recv()

    factor = 1.0 / math.sqrt(half)
    cos = cosine[...]
    sin = sine[...]
    for p in (0, 1):
        gain_r = selected[0:1, p * half : (p + 1) * half]
        gain_i = selected[1:2, p * half : (p + 1) * half]
        denom = jnp.maximum(gain_r * gain_r + gain_i * gain_i, 0.5)
        along_r = gain_r / denom
        along_i = gain_i / denom
        w_r = (cos * along_r - sin * along_i) * factor
        w_i = -(cos * along_i + sin * along_r) * factor
        left = jnp.concatenate([w_r, w_i], axis=0).astype(jnp.bfloat16)
        right = jnp.concatenate([-w_i, w_r], axis=0).astype(jnp.bfloat16)
        result = jnp.dot(left, beam[0, p * half : (p + 1) * half, :], preferred_element_type=jnp.float32)
        result += jnp.dot(right, beam[1, p * half : (p + 1) * half, :], preferred_element_type=jnp.float32)
        result = result.astype(jnp.bfloat16)
        beams_out[0, p, 0] = result[:beams]
        beams_out[0, p, 1] = result[beams:]

    for which in (0, 1):
        for ci in all_chunks:
            for k in masks:
                z_copy(which, k, ci).wait_send()
            for k in range(nf):
                for dg in range(1, ng):
                    y_copy(which, k, ci, dg).wait_send()
    for i in range(nt - 1):
        vis_copy(i).wait_send()
    for iteration in range(ITERS):
        for o in range(len(offsets)):
            update_copy(iteration, o).wait_send()
    for k in masks:
        gain_copy(k).wait_send()


def body(
    voltages,
    prior_gains,
    station_flags,
    ingest_map,
    station_coords,
    pointing,
    corr_channels,
    beam_channels,
):
    nf = lax.axis_size("freq")
    nt = lax.axis_size("tm")
    ng = lax.axis_size("grp")
    _, _, per_input, samples = voltages.shape
    stations = ingest_map.shape[0]
    inputs = 2 * stations
    rows, cols = inputs // ng, inputs // nt
    n_beams = pointing.shape[1] // ng
    step = min(per_input, 64)
    chunks = tuple((part, first, step) for first in range(0, per_input, step) for part in (0, 1))
    nc = len(chunks)
    dma = pltpu.SemaphoreType.DMA
    vmem = pl.BlockSpec(memory_space=pltpu.VMEM)
    vis, gains, beams = pl.pallas_call(
        functools.partial(kernel, nf, nt, ng, chunks),
        out_shape=(
            jax.ShapeDtypeStruct((1, 2, rows, cols), jnp.float32),
            jax.ShapeDtypeStruct((1, 2, inputs), jnp.float32),
            jax.ShapeDtypeStruct((1, 2, 2, n_beams, samples), jnp.bfloat16),
        ),
        in_specs=[vmem] * 6 + [pl.BlockSpec(memory_space=pltpu.SMEM)] * 2,
        out_specs=(vmem, vmem, vmem),
        scratch_shapes=[
            pltpu.VMEM((nf, 2, per_input, samples), jnp.bfloat16),
            pltpu.VMEM((nf, 2, per_input, samples), jnp.bfloat16),
            pltpu.VMEM((stations, LANES), jnp.float32),
            pltpu.VMEM((n_beams, stations), jnp.float32),
            pltpu.VMEM((n_beams, stations), jnp.float32),
            pltpu.VMEM((2, inputs, samples), jnp.bfloat16),
            pltpu.VMEM((2, inputs, samples), jnp.bfloat16),
            pltpu.VMEM((2, rows, inputs), jnp.float32),
            pltpu.VMEM((nt, 2, rows, cols), jnp.bfloat16),
            pltpu.VMEM((nt - 1, 2, rows, cols), jnp.bfloat16),
            pltpu.VMEM((ITERS, ng * nt, 2, rows), jnp.float32),
            pltpu.VMEM((2, inputs), jnp.float32),
            pltpu.VMEM((nf, 2, inputs), jnp.float32),
            dma((2, nf - 1, nc)),
            dma((2, nf - 1, nc)),
            dma((2, ng - 1, nf, nc)),
            dma((2, ng - 1, nf, nc)),
            dma((2,)),
            dma((nt - 1,)),
            dma((nt - 1,)),
            dma((ITERS, ng * nt - 1)),
            dma((ITERS, ng * nt - 1)),
            dma((nf - 1,)),
            dma((nf - 1,)),
        ],
        compiler_params=pltpu.CompilerParams(
            collective_id=0, has_side_effects=True, vmem_limit_bytes=48 * 1024 * 1024
        ),
    )(
        voltages,
        prior_gains,
        station_flags[None],
        ingest_map[None],
        station_coords,
        pointing,
        corr_channels,
        beam_channels,
    )
    return vis, gains, beams


def solution(mesh):
    return jax.shard_map(
        body,
        mesh=mesh,
        in_specs=(
            P(None, None, ("freq", "grp"), "tm"),
            P("freq", None, None),
            P(),
            P(),
            P(),
            P(),
            P(),
            P(),
        ),
        out_specs=(
            P("freq", None, "grp", "tm"),
            P("freq", None, None),
            P("freq", None, None, "grp", "tm"),
        ),
        check_vma=False,
    )
```

```python
import functools
import math

import jax
import jax.numpy as jnp
from jax import lax
from jax.experimental import pallas as pl
from jax.experimental.pallas import tpu as pltpu
from jax.sharding import PartitionSpec as P

ITERS = 4
LANES = 128
grid_cells = 64.0
MESH = pl.DeviceIdType.MESH


def partner(index, mask, count):
    result, bit = 0, 1
    while bit < count:
        digit = (index // bit) % 2
        result = result + bit * ((1 - digit) if mask & bit else digit)
        bit *= 2
    return result


def nt_dot(a, b):
    return lax.dot_general(a, b, (((1,), (1,)), ((), ())), preferred_element_type=jnp.float32)


def kernel(
    nf,
    nt,
    ng,
    chunks,
    windows,
    *refs,
):
    operands, refs = refs[:8], refs[8:]
    (
        vis_out,
        gains_out,
        beams_out,
        src_c,
        src_b,
        keep,
        cosine,
        sine,
        left,
        right,
        mine_beams,
        sent_beams,
        got_beams,
        corr,
        beam,
        gram,
        stage,
        landed,
        updates,
        z,
        gains,
        zs,
        zr,
        ys,
        yr,
        bs,
        br,
        ps,
        pr,
        own_sem,
        vs,
        vr,
        us,
        ur,
        gs,
        gr,
        in_sem,
    ) = refs[:-8]
    held = refs[-8:]
    voltages, prior, flags, slots, coords, pointing, corr_channels, beam_channels = held
    loads = [pltpu.make_async_copy(operands[i], held[i], in_sem.at[i]) for i in range(8)]
    for load in loads:
        load.start()
    f = lax.axis_index("freq")
    t = lax.axis_index("tm")
    g = lax.axis_index("grp")
    _, _, per_input, samples = voltages.shape
    inputs = nf * ng * per_input
    rows = inputs // ng
    cols = inputs // nt
    half = inputs // 2
    offsets = [(dt, dg) for dg in range(ng) for dt in range(nt) if (dt, dg) != (0, 0)]
    masks = list(range(nf - 1, 0, -1))
    peers = {k: partner(f, k, nf) for k in range(nf)}

    def group(dt, dg):
        return {"freq": f, "tm": (t + dt) % nt, "grp": (g + dg) % ng}

    def along_freq(k):
        return {"freq": peers[k], "tm": t, "grp": g}

    barrier = pltpu.get_barrier_semaphore()
    for k in masks:
        pl.semaphore_signal(barrier, inc=1, device_id=along_freq(k), device_id_type=MESH)
    for dt, dg in offsets:
        pl.semaphore_signal(barrier, inc=1, device_id=group(dt, dg), device_id_type=MESH)
    for load in loads:
        load.wait()
    stations = half
    slot_rows = jnp.broadcast_to(slots[...].astype(jnp.float32), (LANES, stations)).T
    flagged = jnp.zeros((stations, LANES), jnp.float32)
    for first in range(0, stations, LANES):
        lane = lax.broadcasted_iota(jnp.int32, (stations, LANES), 1) + first
        flag = flags[0:1, first : first + LANES].astype(jnp.float32)
        flagged += jnp.where(slot_rows == lane.astype(jnp.float32), flag, 0.0)
    flagged = jnp.sum(flagged, axis=1, keepdims=True)
    keep[...] = jnp.broadcast_to(1.0 - flagged, (stations, LANES))

    first_slot = pl.multiple_of(((f * ng + g) * per_input) % stations, per_input)
    kept = keep[pl.ds(first_slot, per_input), 0:1].astype(jnp.bfloat16)

    for k in masks + [0]:
        for part in (0, 1):
            src_c[peers[k], part] = voltages[corr_channels[peers[k]], part] * kept

    pl.semaphore_wait(barrier, len(masks) + len(offsets))
    nw = windows
    width = samples // nw

    def place(owner, chunk):
        part, first, count = chunk
        start = pl.multiple_of((owner * ng + g) * per_input + first, count)
        return corr.at[part, pl.ds(start, count), :]

    def z_copy(k, ci):
        part, first, count = chunks[ci]
        return pltpu.make_async_remote_copy(
            src_ref=src_c.at[peers[k], part, pl.ds(first, count), :],
            dst_ref=place(f, chunks[ci]),
            send_sem=zs.at[k - 1, ci],
            recv_sem=zr.at[k - 1, ci],
            device_id=along_freq(k),
            device_id_type=MESH,
        )

    def y_copy(k, ci, dg):
        part, first, count = chunks[ci]
        spot = place(peers[k], chunks[ci])
        return pltpu.make_async_remote_copy(
            src_ref=src_c.at[f, part, pl.ds(first, count), :] if k == 0 else spot,
            dst_ref=spot,
            send_sem=ys.at[dg - 1, k, ci],
            recv_sem=yr.at[dg - 1, k, ci],
            device_id=group(0, dg),
            device_id_type=MESH,
        )

    def forward(k, ci):
        for dg in range(1, ng):
            y_copy(k, ci, dg).start()

    def block(owner, member):
        return pl.ds(pl.multiple_of((owner * ng + member) * per_input, per_input), per_input)

    own_copy = pltpu.make_async_copy(src_c.at[f], corr.at[:, block(f, g), :], own_sem)

    def b_copy(k, w):
        return pltpu.make_async_remote_copy(
            src_ref=src_b.at[peers[k], w],
            dst_ref=beam.at[w, :, block(f, g), :],
            send_sem=bs.at[k - 1, w],
            recv_sem=br.at[k - 1, w],
            device_id=along_freq(k),
            device_id_type=MESH,
        )

    def p_copy(dg, w):
        return pltpu.make_async_remote_copy(
            src_ref=sent_beams.at[dg - 1, w],
            dst_ref=got_beams.at[dg - 1, w],
            send_sem=ps.at[dg - 1, w],
            recv_sem=pr.at[dg - 1, w],
            device_id=group(0, dg),
            device_id_type=MESH,
        )

    def pick_beams():
        for w in range(nw):
            for k in masks + [0]:
                for part in (0, 1):
                    picked = voltages[beam_channels[peers[k]], part, :, w * width : (w + 1) * width] * kept
                    if k == 0:
                        beam[w, part, block(f, g), :] = picked
                    else:
                        src_b[peers[k], w, part] = picked

    def clear_others():
        for w in range(nw):
            for owner in range(nf):
                for dg in range(1, ng):
                    for part in (0, 1):
                        beam[w, part, block(owner, (g + dg) % ng), :] = jnp.zeros((per_input, width), jnp.bfloat16)

    n_beams = cosine.shape[0]
    beams = n_beams // ng
    my_beam = beam_channels[f]

    def point_phases():
        ratio = 0.875 + 0.25 * (my_beam.astype(jnp.float32) + 0.5) / nf
        east_dir, north_dir = (
            jnp.broadcast_to((pointing[d : d + 1, :].astype(jnp.float32) + 0.5) / grid_cells - 0.5, (LANES, n_beams)).T
            for d in (0, 1)
        )
        east, north = (jnp.broadcast_to(coords[d : d + 1, :], (LANES, stations)).T for d in (0, 1))
        station = lax.broadcasted_iota(jnp.int32, (stations, LANES), 0)
        for first in range(0, stations, LANES):
            lanes = slice(first, first + LANES)
            match = station == slots[0:1, lanes]
            slot_east = jnp.sum(jnp.where(match, east, 0.0), axis=0, keepdims=True)
            slot_north = jnp.sum(jnp.where(match, north, 0.0), axis=0, keepdims=True)
            phase = 2.0 * math.pi * ratio * (east_dir * slot_east + north_dir * slot_north)
            cosine[:, lanes] = jnp.cos(phase)
            sine[:, lanes] = jnp.sin(phase)

    all_chunks = range(len(chunks))
    for ci in all_chunks:
        for k in masks:
            z_copy(k, ci).start()
    for ci in all_chunks:
        forward(0, ci)
    own_copy.start()
    pick_beams()
    for w in range(nw):
        for k in masks:
            b_copy(k, w).start()
    clear_others()
    point_phases()
    for ci in all_chunks:
        for k in masks:
            z_copy(k, ci).wait_recv()
            forward(k, ci)
    own_copy.wait()
    for ci in all_chunks:
        for k in range(nf):
            for dg in range(1, ng):
                y_copy(k, ci, dg).wait_recv()

    scale = 1.0 / (samples * nt)
    row_start = pl.multiple_of(g * rows, rows)

    def vis_copy(i):
        return pltpu.make_async_remote_copy(
            src_ref=stage.at[i],
            dst_ref=landed.at[i],
            send_sem=vs.at[i],
            recv_sem=vr.at[i],
            device_id=group(i + 1, 0),
            device_id_type=MESH,
        )

    def correlate(i, carry):
        j = (t + 1 + i) % nt
        tile = pl.ds(pl.multiple_of(j * cols, cols), cols)
        mine_r = corr[0, pl.ds(row_start, rows), :]
        mine_i = corr[1, pl.ds(row_start, rows), :]
        other_r = corr[0, tile, :]
        other_i = corr[1, tile, :]
        real = (nt_dot(mine_r, other_r) + nt_dot(mine_i, other_i)) * scale
        imag = (nt_dot(mine_i, other_r) - nt_dot(mine_r, other_i)) * scale
        gram[0, :, tile] = real
        gram[1, :, tile] = imag

        @pl.when(i < nt - 1)
        def _():
            stage[i, 0] = real.astype(jnp.bfloat16)
            stage[i, 1] = imag.astype(jnp.bfloat16)
            vis_copy(i).start()

        return carry

    lax.fori_loop(0, nt, correlate, 0)

    z[...] = prior[0]
    slot = g * nt + t
    strip = LANES

    def update_copy(iteration, o):
        dt, dg = offsets[o]
        return pltpu.make_async_remote_copy(
            src_ref=updates.at[iteration, slot],
            dst_ref=updates.at[iteration, slot],
            send_sem=us.at[iteration, o],
            recv_sem=ur.at[iteration, o],
            device_id=group(dt, dg),
            device_id_type=MESH,
        )

    for iteration in range(ITERS):
        power = jnp.sum(z[...] * z[...]) + 1e-06

        def product(r, carry):
            here = pl.ds(pl.multiple_of(r * strip, strip), strip)
            total_r = jnp.zeros((strip, LANES), jnp.float32)
            total_i = jnp.zeros((strip, LANES), jnp.float32)
            for c in range(inputs // LANES):
                lanes = slice(c * LANES, (c + 1) * LANES)
                part_r = gram[0, here, lanes]
                part_i = gram[1, here, lanes]
                gain_r = z[0:1, lanes]
                gain_i = z[1:2, lanes]
                total_r += part_r * gain_r - part_i * gain_i
                total_i += part_i * gain_r + part_r * gain_i
            updates[iteration, slot, 0:1, here] = jnp.sum(total_r.T, axis=0, keepdims=True)
            updates[iteration, slot, 1:2, here] = jnp.sum(total_i.T, axis=0, keepdims=True)
            return carry

        lax.fori_loop(0, rows // strip, product, 0)
        for o in range(len(offsets)):
            update_copy(iteration, o).start()
        for o in range(len(offsets)):
            update_copy(iteration, o).wait_recv()
        for h in range(ng):
            total = updates[iteration, h * nt]
            for other in range(1, nt):
                total = total + updates[iteration, h * nt + other]
            lanes = slice(h * rows, (h + 1) * rows)
            z[:, lanes] = 0.5 * (z[:, lanes] + inputs * total / power)

    gains[f] = z[...]
    gains_out[0] = z[...]

    def gain_copy(k):
        return pltpu.make_async_remote_copy(
            src_ref=gains.at[f],
            dst_ref=gains.at[f],
            send_sem=gs.at[k - 1],
            recv_sem=gr.at[k - 1],
            device_id=along_freq(k),
            device_id_type=MESH,
        )

    for k in masks:
        gain_copy(k).start()
    for i in range(nt - 1):
        vis_copy(i).wait_recv()
    own_tile = pl.ds(pl.multiple_of(t * cols, cols), cols)
    for part in (0, 1):
        total = gram[part, :, own_tile]
        for i in range(nt - 1):
            total = total + landed[i, part].astype(jnp.float32)
        vis_out[0, part] = total

    for k in masks:
        gain_copy(k).wait_recv()
    selected = jnp.zeros_like(z)
    for k in range(nf):
        selected = selected + jnp.where(corr_channels[k] == my_beam, 1.0, 0.0) * gains[k]

    factor = 1.0 / math.sqrt(half)
    for p in (0, 1):
        gain_r = selected[0:1, p * half : (p + 1) * half]
        gain_i = selected[1:2, p * half : (p + 1) * half]
        denom = jnp.maximum(gain_r * gain_r + gain_i * gain_i, 0.5)
        along_r = gain_r / denom
        along_i = gain_i / denom
        for h in range(ng):
            span = slice(h * beams, (h + 1) * beams)
            cos = cosine[span, :]
            sin = sine[span, :]
            w_r = ((cos * along_r - sin * along_i) * factor).astype(jnp.bfloat16)
            w_i = (-(cos * along_i + sin * along_r) * factor).astype(jnp.bfloat16)
            left[p, h, 0:beams] = w_r
            left[p, h, beams:] = w_i
            right[p, h, 0:beams] = -w_i
            right[p, h, beams:] = w_r

    def beamform(p, w, side):
        rows_p = slice(p * half, (p + 1) * half)
        result = jnp.dot(left[p, side], beam[w, 0, rows_p, :], preferred_element_type=jnp.float32)
        return result + jnp.dot(right[p, side], beam[w, 1, rows_p, :], preferred_element_type=jnp.float32)

    for w in range(nw):
        for k in masks:
            b_copy(k, w).wait_recv()
        for dg in range(1, ng):
            for p in (0, 1):
                sent_beams[dg - 1, w, p] = beamform(p, w, (g + dg) % ng).astype(jnp.bfloat16)
            p_copy(dg, w).start()
        for p in (0, 1):
            mine_beams[w, p] = beamform(p, w, g)

    for w in range(nw):
        lanes = slice(w * width, (w + 1) * width)
        for dg in range(1, ng):
            p_copy(dg, w).wait_recv()
        for p in (0, 1):
            total = mine_beams[w, p]
            for dg in range(1, ng):
                total = total + got_beams[dg - 1, w, p].astype(jnp.float32)
            total = total.astype(jnp.bfloat16)
            beams_out[0, p, 0, :, lanes] = total[:beams]
            beams_out[0, p, 1, :, lanes] = total[beams:]

    for ci in all_chunks:
        for k in masks:
            z_copy(k, ci).wait_send()
        for k in range(nf):
            for dg in range(1, ng):
                y_copy(k, ci, dg).wait_send()
    for w in range(nw):
        for k in masks:
            b_copy(k, w).wait_send()
        for dg in range(1, ng):
            p_copy(dg, w).wait_send()
    for i in range(nt - 1):
        vis_copy(i).wait_send()
    for iteration in range(ITERS):
        for o in range(len(offsets)):
            update_copy(iteration, o).wait_send()
    for k in masks:
        gain_copy(k).wait_send()


def body(
    voltages,
    prior_gains,
    station_flags,
    ingest_map,
    station_coords,
    pointing,
    corr_channels,
    beam_channels,
):
    nf = lax.axis_size("freq")
    nt = lax.axis_size("tm")
    ng = lax.axis_size("grp")
    _, _, per_input, samples = voltages.shape
    stations = ingest_map.shape[0]
    inputs = 2 * stations
    rows, cols = inputs // ng, inputs // nt
    n_beams = pointing.shape[1]
    part_beams = n_beams // ng
    nw = 4
    width = samples // nw
    step = min(per_input, 32)
    chunks = tuple((part, first, step) for first in range(0, per_input, step) for part in (0, 1))
    nc = len(chunks)
    dma = pltpu.SemaphoreType.DMA
    vmem = pl.BlockSpec(memory_space=pltpu.VMEM)
    vis, gains, beams = pl.pallas_call(
        functools.partial(kernel, nf, nt, ng, chunks, nw),
        out_shape=(
            jax.ShapeDtypeStruct((1, 2, rows, cols), jnp.float32),
            jax.ShapeDtypeStruct((1, 2, inputs), jnp.float32),
            jax.ShapeDtypeStruct((1, 2, 2, part_beams, samples), jnp.bfloat16),
        ),
        in_specs=[pl.BlockSpec(memory_space=pltpu.HBM)] * 8,
        out_specs=(vmem, vmem, vmem),
        scratch_shapes=[
            pltpu.VMEM((nf, 2, per_input, samples), jnp.bfloat16),
            pltpu.VMEM((nf, nw, 2, per_input, width), jnp.bfloat16),
            pltpu.VMEM((stations, LANES), jnp.float32),
            pltpu.VMEM((n_beams, stations), jnp.float32),
            pltpu.VMEM((n_beams, stations), jnp.float32),
            pltpu.VMEM((2, ng, 2 * part_beams, stations), jnp.bfloat16),
            pltpu.VMEM((2, ng, 2 * part_beams, stations), jnp.bfloat16),
            pltpu.VMEM((nw, 2, 2 * part_beams, width), jnp.float32),
            pltpu.VMEM((ng - 1, nw, 2, 2 * part_beams, width), jnp.bfloat16),
            pltpu.VMEM((ng - 1, nw, 2, 2 * part_beams, width), jnp.bfloat16),
            pltpu.VMEM((2, inputs, samples), jnp.bfloat16),
            pltpu.VMEM((nw, 2, inputs, width), jnp.bfloat16),
            pltpu.VMEM((2, rows, inputs), jnp.float32),
            pltpu.VMEM((nt, 2, rows, cols), jnp.bfloat16),
            pltpu.VMEM((nt - 1, 2, rows, cols), jnp.bfloat16),
            pltpu.VMEM((ITERS, ng * nt, 2, rows), jnp.float32),
            pltpu.VMEM((2, inputs), jnp.float32),
            pltpu.VMEM((nf, 2, inputs), jnp.float32),
            dma((nf - 1, nc)),
            dma((nf - 1, nc)),
            dma((ng - 1, nf, nc)),
            dma((ng - 1, nf, nc)),
            dma((nf - 1, nw)),
            dma((nf - 1, nw)),
            dma((ng - 1, nw)),
            dma((ng - 1, nw)),
            dma,
            dma((nt - 1,)),
            dma((nt - 1,)),
            dma((ITERS, ng * nt - 1)),
            dma((ITERS, ng * nt - 1)),
            dma((nf - 1,)),
            dma((nf - 1,)),
            dma((8,)),
            pltpu.VMEM(voltages.shape, jnp.bfloat16),
            pltpu.VMEM(prior_gains.shape, jnp.float32),
            pltpu.VMEM((1, stations), jnp.int32),
            pltpu.VMEM((1, stations), jnp.int32),
            pltpu.VMEM(station_coords.shape, jnp.float32),
            pltpu.VMEM(pointing.shape, jnp.int32),
            pltpu.SMEM(corr_channels.shape, jnp.int32),
            pltpu.SMEM(beam_channels.shape, jnp.int32),
        ],
        compiler_params=pltpu.CompilerParams(
            collective_id=0, has_side_effects=True, vmem_limit_bytes=48 * 1024 * 1024
        ),
    )(
        voltages,
        prior_gains,
        station_flags[None],
        ingest_map[None],
        station_coords,
        pointing,
        corr_channels,
        beam_channels,
    )
    return vis, gains, beams


def solution(mesh):
    return jax.shard_map(
        body,
        mesh=mesh,
        in_specs=(
            P(None, None, ("freq", "grp"), "tm"),
            P("freq", None, None),
            P(),
            P(),
            P(),
            P(),
            P(),
            P(),
        ),
        out_specs=(
            P("freq", None, "grp", "tm"),
            P("freq", None, None),
            P("freq", None, None, "grp", "tm"),
        ),
        check_vma=False,
    )
```

```python
import functools
import math

import jax
import jax.numpy as jnp
from jax import lax
from jax.experimental import pallas as pl
from jax.experimental.pallas import tpu as pltpu
from jax.sharding import PartitionSpec as P

ITERS = 4
LANES = 128
grid_cells = 64.0
MESH = pl.DeviceIdType.MESH


def partner(index, mask, count):
    result, bit = 0, 1
    while bit < count:
        digit = (index // bit) % 2
        result = result + bit * ((1 - digit) if mask & bit else digit)
        bit *= 2
    return result


def nt_dot(a, b):
    return lax.dot_general(a, b, (((1,), (1,)), ((), ())), preferred_element_type=jnp.float32)


def kernel(
    nf,
    nt,
    ng,
    chunks,
    windows,
    *refs,
):
    operands, refs = refs[:8], refs[8:]
    (
        vis_out,
        gains_out,
        beams_out,
        src_c,
        src_b,
        keep,
        cosine,
        sine,
        left,
        right,
        mine_beams,
        sent_beams,
        got_beams,
        corr,
        beam,
        gram,
        stage,
        landed,
        updates,
        z,
        gains,
        zs,
        zr,
        ys,
        yr,
        bs,
        br,
        ps,
        pr,
        own_sem,
        vs,
        vr,
        us,
        ur,
        gs,
        gr,
        in_sem,
    ) = refs[:-8]
    held = refs[-8:]
    voltages, prior, flags, slots, coords, pointing, corr_channels, beam_channels = held
    loads = [pltpu.make_async_copy(operands[i], held[i], in_sem.at[i]) for i in range(8)]
    for load in loads:
        load.start()
    f = lax.axis_index("freq")
    t = lax.axis_index("tm")
    g = lax.axis_index("grp")
    _, _, per_input, samples = voltages.shape
    inputs = nf * ng * per_input
    rows = inputs // ng
    cols = inputs // nt
    half = inputs // 2
    offsets = [(dt, dg) for dg in range(ng) for dt in range(nt) if (dt, dg) != (0, 0)]
    masks = list(range(nf - 1, 0, -1))
    peers = {k: partner(f, k, nf) for k in range(nf)}

    def group(dt, dg):
        return {"freq": f, "tm": (t + dt) % nt, "grp": (g + dg) % ng}

    def along_freq(k):
        return {"freq": peers[k], "tm": t, "grp": g}

    barrier = pltpu.get_barrier_semaphore()
    for k in masks:
        pl.semaphore_signal(barrier, inc=1, device_id=along_freq(k), device_id_type=MESH)
    for dt, dg in offsets:
        pl.semaphore_signal(barrier, inc=1, device_id=group(dt, dg), device_id_type=MESH)
    for load in loads:
        load.wait()
    stations = half
    slot_rows = jnp.broadcast_to(slots[...].astype(jnp.float32), (LANES, stations)).T
    flagged = jnp.zeros((stations, LANES), jnp.float32)
    for first in range(0, stations, LANES):
        lane = lax.broadcasted_iota(jnp.int32, (stations, LANES), 1) + first
        flag = flags[0:1, first : first + LANES].astype(jnp.float32)
        flagged += jnp.where(slot_rows == lane.astype(jnp.float32), flag, 0.0)
    flagged = jnp.sum(flagged, axis=1, keepdims=True)
    keep[...] = jnp.broadcast_to(1.0 - flagged, (stations, LANES))

    first_slot = pl.multiple_of(((f * ng + g) * per_input) % stations, per_input)
    kept = keep[pl.ds(first_slot, per_input), 0:1].astype(jnp.bfloat16)

    for k in masks + [0]:
        for part in (0, 1):
            src_c[peers[k], part] = voltages[corr_channels[peers[k]], part] * kept

    pl.semaphore_wait(barrier, len(masks) + len(offsets))
    nw = windows
    width = samples // nw

    def place(owner, chunk):
        part, first, count = chunk
        start = pl.multiple_of((owner * ng + g) * per_input + first, count)
        return corr.at[part, pl.ds(start, count), :]

    def z_copy(k, ci):
        part, first, count = chunks[ci]
        return pltpu.make_async_remote_copy(
            src_ref=src_c.at[peers[k], part, pl.ds(first, count), :],
            dst_ref=place(f, chunks[ci]),
            send_sem=zs.at[k - 1, ci],
            recv_sem=zr.at[k - 1, ci],
            device_id=along_freq(k),
            device_id_type=MESH,
        )

    def y_copy(k, ci, dg):
        part, first, count = chunks[ci]
        spot = place(peers[k], chunks[ci])
        return pltpu.make_async_remote_copy(
            src_ref=src_c.at[f, part, pl.ds(first, count), :] if k == 0 else spot,
            dst_ref=spot,
            send_sem=ys.at[dg - 1, k, ci],
            recv_sem=yr.at[dg - 1, k, ci],
            device_id=group(0, dg),
            device_id_type=MESH,
        )

    def forward(k, ci):
        for dg in range(1, ng):
            y_copy(k, ci, dg).start()

    def block(owner, member):
        return pl.ds(pl.multiple_of((owner * ng + member) * per_input, per_input), per_input)

    own_copy = pltpu.make_async_copy(src_c.at[f], corr.at[:, block(f, g), :], own_sem)

    def b_copy(k, w):
        return pltpu.make_async_remote_copy(
            src_ref=src_b.at[peers[k], w],
            dst_ref=beam.at[w, :, block(f, g), :],
            send_sem=bs.at[k - 1, w],
            recv_sem=br.at[k - 1, w],
            device_id=along_freq(k),
            device_id_type=MESH,
        )

    def p_copy(dg, w):
        return pltpu.make_async_remote_copy(
            src_ref=sent_beams.at[dg - 1, w],
            dst_ref=got_beams.at[dg - 1, w],
            send_sem=ps.at[dg - 1, w],
            recv_sem=pr.at[dg - 1, w],
            device_id=group(0, dg),
            device_id_type=MESH,
        )

    def pick_beams():
        for w in range(nw):
            for k in masks + [0]:
                for part in (0, 1):
                    picked = voltages[beam_channels[peers[k]], part, :, w * width : (w + 1) * width] * kept
                    if k == 0:
                        beam[w, part, block(f, g), :] = picked
                    else:
                        src_b[peers[k], w, part] = picked

    def clear_others():
        for w in range(nw):
            for owner in range(nf):
                for dg in range(1, ng):
                    for part in (0, 1):
                        beam[w, part, block(owner, (g + dg) % ng), :] = jnp.zeros((per_input, width), jnp.bfloat16)

    n_beams = cosine.shape[0]
    beams = n_beams // ng
    my_beam = beam_channels[f]

    def point_phases():
        ratio = 0.875 + 0.25 * (my_beam.astype(jnp.float32) + 0.5) / nf
        east_dir, north_dir = (
            jnp.broadcast_to((pointing[d : d + 1, :].astype(jnp.float32) + 0.5) / grid_cells - 0.5, (LANES, n_beams)).T
            for d in (0, 1)
        )
        east, north = (jnp.broadcast_to(coords[d : d + 1, :], (LANES, stations)).T for d in (0, 1))
        station = lax.broadcasted_iota(jnp.int32, (stations, LANES), 0)
        for first in range(0, stations, LANES):
            lanes = slice(first, first + LANES)
            match = station == slots[0:1, lanes]
            slot_east = jnp.sum(jnp.where(match, east, 0.0), axis=0, keepdims=True)
            slot_north = jnp.sum(jnp.where(match, north, 0.0), axis=0, keepdims=True)
            phase = 2.0 * math.pi * ratio * (east_dir * slot_east + north_dir * slot_north)
            cosine[:, lanes] = jnp.cos(phase)
            sine[:, lanes] = jnp.sin(phase)

    all_chunks = range(len(chunks))
    for ci in all_chunks:
        for k in masks:
            z_copy(k, ci).start()
    for ci in all_chunks:
        forward(0, ci)
    own_copy.start()
    pick_beams()
    early = (5 * nw) // 8
    for w in range(early):
        for k in masks:
            b_copy(k, w).start()
    clear_others()
    point_phases()
    for ci in all_chunks:
        for k in masks:
            z_copy(k, ci).wait_recv()
            forward(k, ci)
    own_copy.wait()
    for ci in all_chunks:
        for k in range(nf):
            for dg in range(1, ng):
                y_copy(k, ci, dg).wait_recv()

    scale = 1.0 / (samples * nt)
    row_start = pl.multiple_of(g * rows, rows)

    def vis_copy(i):
        return pltpu.make_async_remote_copy(
            src_ref=stage.at[i],
            dst_ref=landed.at[i],
            send_sem=vs.at[i],
            recv_sem=vr.at[i],
            device_id=group(i + 1, 0),
            device_id_type=MESH,
        )

    def correlate(i, carry):
        j = (t + 1 + i) % nt
        tile = pl.ds(pl.multiple_of(j * cols, cols), cols)
        mine_r = corr[0, pl.ds(row_start, rows), :]
        mine_i = corr[1, pl.ds(row_start, rows), :]
        other_r = corr[0, tile, :]
        other_i = corr[1, tile, :]
        real = (nt_dot(mine_r, other_r) + nt_dot(mine_i, other_i)) * scale
        imag = (nt_dot(mine_i, other_r) - nt_dot(mine_r, other_i)) * scale
        gram[0, :, tile] = real
        gram[1, :, tile] = imag

        @pl.when(i < nt - 1)
        def _():
            stage[i, 0] = real.astype(jnp.bfloat16)
            stage[i, 1] = imag.astype(jnp.bfloat16)

        return carry

    lax.fori_loop(0, nt, correlate, 0)

    z[...] = prior[0]
    slot = g * nt + t
    strip = LANES

    def update_copy(iteration, o):
        dt, dg = offsets[o]
        return pltpu.make_async_remote_copy(
            src_ref=updates.at[iteration, slot],
            dst_ref=updates.at[iteration, slot],
            send_sem=us.at[iteration, o],
            recv_sem=ur.at[iteration, o],
            device_id=group(dt, dg),
            device_id_type=MESH,
        )

    for iteration in range(ITERS):
        power = jnp.sum(z[...] * z[...]) + 1e-06

        def product(r, carry):
            here = pl.ds(pl.multiple_of(r * strip, strip), strip)
            total_r = jnp.zeros((strip, LANES), jnp.float32)
            total_i = jnp.zeros((strip, LANES), jnp.float32)
            for c in range(inputs // LANES):
                lanes = slice(c * LANES, (c + 1) * LANES)
                part_r = gram[0, here, lanes]
                part_i = gram[1, here, lanes]
                gain_r = z[0:1, lanes]
                gain_i = z[1:2, lanes]
                total_r += part_r * gain_r - part_i * gain_i
                total_i += part_i * gain_r + part_r * gain_i
            updates[iteration, slot, 0:1, here] = jnp.sum(total_r.T, axis=0, keepdims=True)
            updates[iteration, slot, 1:2, here] = jnp.sum(total_i.T, axis=0, keepdims=True)
            return carry

        lax.fori_loop(0, rows // strip, product, 0)
        for o in range(len(offsets)):
            update_copy(iteration, o).start()
        if iteration == ITERS - 1:
            for i in range(nt - 1):
                vis_copy(i).start()
        for o in range(len(offsets)):
            update_copy(iteration, o).wait_recv()
        for h in range(ng):
            total = updates[iteration, h * nt]
            for other in range(1, nt):
                total = total + updates[iteration, h * nt + other]
            lanes = slice(h * rows, (h + 1) * rows)
            z[:, lanes] = 0.5 * (z[:, lanes] + inputs * total / power)

    gains[f] = z[...]
    gains_out[0] = z[...]

    def gain_copy(k):
        return pltpu.make_async_remote_copy(
            src_ref=gains.at[f],
            dst_ref=gains.at[f],
            send_sem=gs.at[k - 1],
            recv_sem=gr.at[k - 1],
            device_id=along_freq(k),
            device_id_type=MESH,
        )

    for k in masks:
        gain_copy(k).start()
    for w in range(early, nw):
        for k in masks:
            b_copy(k, w).start()
    for k in masks:
        gain_copy(k).wait_recv()
    selected = jnp.zeros_like(z)
    for k in range(nf):
        selected = selected + jnp.where(corr_channels[k] == my_beam, 1.0, 0.0) * gains[k]

    factor = 1.0 / math.sqrt(half)
    for p in (0, 1):
        gain_r = selected[0:1, p * half : (p + 1) * half]
        gain_i = selected[1:2, p * half : (p + 1) * half]
        denom = jnp.maximum(gain_r * gain_r + gain_i * gain_i, 0.5)
        along_r = gain_r / denom
        along_i = gain_i / denom
        for h in range(ng):
            span = slice(h * beams, (h + 1) * beams)
            cos = cosine[span, :]
            sin = sine[span, :]
            w_r = ((cos * along_r - sin * along_i) * factor).astype(jnp.bfloat16)
            w_i = (-(cos * along_i + sin * along_r) * factor).astype(jnp.bfloat16)
            left[p, h, 0:beams] = w_r
            left[p, h, beams:] = w_i
            right[p, h, 0:beams] = -w_i
            right[p, h, beams:] = w_r

    def beamform(p, w, side):
        rows_p = slice(p * half, (p + 1) * half)
        result = jnp.dot(left[p, side], beam[w, 0, rows_p, :], preferred_element_type=jnp.float32)
        return result + jnp.dot(right[p, side], beam[w, 1, rows_p, :], preferred_element_type=jnp.float32)

    for w in range(nw):
        for k in masks:
            b_copy(k, w).wait_recv()
        for dg in range(1, ng):
            for p in (0, 1):
                sent_beams[dg - 1, w, p] = beamform(p, w, (g + dg) % ng).astype(jnp.bfloat16)
            p_copy(dg, w).start()
        for p in (0, 1):
            mine_beams[w, p] = beamform(p, w, g)

    for i in range(nt - 1):
        vis_copy(i).wait_recv()
    own_tile = pl.ds(pl.multiple_of(t * cols, cols), cols)
    for part in (0, 1):
        total = gram[part, :, own_tile]
        for i in range(nt - 1):
            total = total + landed[i, part].astype(jnp.float32)
        vis_out[0, part] = total

    for w in range(nw):
        lanes = slice(w * width, (w + 1) * width)
        for dg in range(1, ng):
            p_copy(dg, w).wait_recv()
        for p in (0, 1):
            total = mine_beams[w, p]
            for dg in range(1, ng):
                total = total + got_beams[dg - 1, w, p].astype(jnp.float32)
            total = total.astype(jnp.bfloat16)
            beams_out[0, p, 0, :, lanes] = total[:beams]
            beams_out[0, p, 1, :, lanes] = total[beams:]

    for ci in all_chunks:
        for k in masks:
            z_copy(k, ci).wait_send()
        for k in range(nf):
            for dg in range(1, ng):
                y_copy(k, ci, dg).wait_send()
    for w in range(nw):
        for k in masks:
            b_copy(k, w).wait_send()
        for dg in range(1, ng):
            p_copy(dg, w).wait_send()
    for i in range(nt - 1):
        vis_copy(i).wait_send()
    for iteration in range(ITERS):
        for o in range(len(offsets)):
            update_copy(iteration, o).wait_send()
    for k in masks:
        gain_copy(k).wait_send()


def body(
    voltages,
    prior_gains,
    station_flags,
    ingest_map,
    station_coords,
    pointing,
    corr_channels,
    beam_channels,
):
    nf = lax.axis_size("freq")
    nt = lax.axis_size("tm")
    ng = lax.axis_size("grp")
    _, _, per_input, samples = voltages.shape
    stations = ingest_map.shape[0]
    inputs = 2 * stations
    rows, cols = inputs // ng, inputs // nt
    n_beams = pointing.shape[1]
    part_beams = n_beams // ng
    nw = 8
    width = samples // nw
    step = min(per_input, 32)
    chunks = tuple((part, first, step) for first in range(0, per_input, step) for part in (0, 1))
    nc = len(chunks)
    dma = pltpu.SemaphoreType.DMA
    vmem = pl.BlockSpec(memory_space=pltpu.VMEM)
    vis, gains, beams = pl.pallas_call(
        functools.partial(kernel, nf, nt, ng, chunks, nw),
        out_shape=(
            jax.ShapeDtypeStruct((1, 2, rows, cols), jnp.float32),
            jax.ShapeDtypeStruct((1, 2, inputs), jnp.float32),
            jax.ShapeDtypeStruct((1, 2, 2, part_beams, samples), jnp.bfloat16),
        ),
        in_specs=[pl.BlockSpec(memory_space=pltpu.HBM)] * 8,
        out_specs=(vmem, vmem, vmem),
        scratch_shapes=[
            pltpu.VMEM((nf, 2, per_input, samples), jnp.bfloat16),
            pltpu.VMEM((nf, nw, 2, per_input, width), jnp.bfloat16),
            pltpu.VMEM((stations, LANES), jnp.float32),
            pltpu.VMEM((n_beams, stations), jnp.float32),
            pltpu.VMEM((n_beams, stations), jnp.float32),
            pltpu.VMEM((2, ng, 2 * part_beams, stations), jnp.bfloat16),
            pltpu.VMEM((2, ng, 2 * part_beams, stations), jnp.bfloat16),
            pltpu.VMEM((nw, 2, 2 * part_beams, width), jnp.float32),
            pltpu.VMEM((ng - 1, nw, 2, 2 * part_beams, width), jnp.bfloat16),
            pltpu.VMEM((ng - 1, nw, 2, 2 * part_beams, width), jnp.bfloat16),
            pltpu.VMEM((2, inputs, samples), jnp.bfloat16),
            pltpu.VMEM((nw, 2, inputs, width), jnp.bfloat16),
            pltpu.VMEM((2, rows, inputs), jnp.float32),
            pltpu.VMEM((nt, 2, rows, cols), jnp.bfloat16),
            pltpu.VMEM((nt - 1, 2, rows, cols), jnp.bfloat16),
            pltpu.VMEM((ITERS, ng * nt, 2, rows), jnp.float32),
            pltpu.VMEM((2, inputs), jnp.float32),
            pltpu.VMEM((nf, 2, inputs), jnp.float32),
            dma((nf - 1, nc)),
            dma((nf - 1, nc)),
            dma((ng - 1, nf, nc)),
            dma((ng - 1, nf, nc)),
            dma((nf - 1, nw)),
            dma((nf - 1, nw)),
            dma((ng - 1, nw)),
            dma((ng - 1, nw)),
            dma,
            dma((nt - 1,)),
            dma((nt - 1,)),
            dma((ITERS, ng * nt - 1)),
            dma((ITERS, ng * nt - 1)),
            dma((nf - 1,)),
            dma((nf - 1,)),
            dma((8,)),
            pltpu.VMEM(voltages.shape, jnp.bfloat16),
            pltpu.VMEM(prior_gains.shape, jnp.float32),
            pltpu.VMEM((1, stations), jnp.int32),
            pltpu.VMEM((1, stations), jnp.int32),
            pltpu.VMEM(station_coords.shape, jnp.float32),
            pltpu.VMEM(pointing.shape, jnp.int32),
            pltpu.SMEM(corr_channels.shape, jnp.int32),
            pltpu.SMEM(beam_channels.shape, jnp.int32),
        ],
        compiler_params=pltpu.CompilerParams(
            collective_id=0, has_side_effects=True, vmem_limit_bytes=67043328
        ),
    )(
        voltages,
        prior_gains,
        station_flags[None],
        ingest_map[None],
        station_coords,
        pointing,
        corr_channels,
        beam_channels,
    )
    return vis, gains, beams


def solution(mesh):
    return jax.shard_map(
        body,
        mesh=mesh,
        in_specs=(
            P(None, None, ("freq", "grp"), "tm"),
            P("freq", None, None),
            P(),
            P(),
            P(),
            P(),
            P(),
            P(),
        ),
        out_specs=(
            P("freq", None, "grp", "tm"),
            P("freq", None, None),
            P("freq", None, None, "grp", "tm"),
        ),
        check_vma=False,
    )
```
